128 devices in a mesh: space: 32 (over y, z, core), dp: 4 (over x).
Axes of the slice: x: 4, y: 4, z: 4, core: 2. Of those that a mesh axis runs over, the one named last changes fastest.
Arguments:
- forcing: bfloat16 [4, 512, 16, 8, 128], P('dp', 'space'), may hold values from -6 to 6
- hidden_prev: bfloat16 [4, 512, 64, 8, 128], P('dp', 'space'), may hold values from -0.8984375 to 0.8984375
- cell_prev: bfloat16 [4, 512, 64, 8, 128], P('dp', 'space'), may hold values from -4 to 4
- hidden_grad: bfloat16 [4, 512, 64, 8, 128], P('dp', 'space'), may hold values from -0.03125 to 0.03125
- w_gates: bfloat16 [256, 720], replicated, may hold values from -0.21875 to 0.21875
- gate_bias: float32 [256], replicated, may hold values from -4 to 4
- worker: int32 [4, 512], P('dp'), may hold values from -1 to 31, as said below
Outputs:
- hidden_next: bfloat16 [4, 512, 64, 8, 128], P('dp', 'space')
- cell_next: bfloat16 [4, 512, 64, 8, 128], P('dp', 'space')
- weight_grad: float32 [256, 720], P('space')
- bias_grad: float32 [256], P('space')
The draws below stay inside these ranges and needn't reach their ends.
Inputs may be any that keep to these rules, and one draw needn't show every extreme that they name: Each year's active tiles (worker >= 0) are dealt to workers in increasing tile order: the j-th active tile, from 0, goes to worker j modulo the number of devices along space; every year has exactly 8 active tiles for every worker, one home in every year has all 16 of its tiles active, and so at most 1 tiles, reached, go from one home to one worker.
All inputs are finite; a program needn't handle non-finite values.
Results may differ from the reference program's by a relative error of at most 0.0075.
Values may be sent and summed in bfloat16 or wider, within the bound.
No kernel may reach another device: no remote copies, remote signals or barrier semaphores. Data moves between devices by JAX's collectives and lax.ppermute only.
A program may use at most 64 MiB of HBM per device.

```python
import jax
import jax.numpy as jnp
from jax import lax

CIN = 16
HID = 64
TILE_ROWS = 8
TILE_COLS = 128
TW = 4
KIN = 80
GATES = 256
TH = 16
CAP = 8
TILES = 512
YEARS = 4


def draw_worker(key, part):
    homes = TILES // TH

    def one_year(year_key):
        key_order, key_count, key_pick = jax.random.split(year_key, 3)
        order = jax.random.permutation(key_order, homes)
        values = jax.random.randint(key_count, (homes // 2,), 0, TH + 1)
        values = values.at[0].set(TH)
        paired = jnp.stack([values, TH - values], axis=1).reshape(homes)
        counts = jnp.zeros((homes,), jnp.int32).at[order].set(paired.astype(jnp.int32))
        scores = jax.random.randint(key_pick, (homes, TH), 0, 1 << 20) * TH + jnp.arange(TH)[None, :]
        placed = jnp.argsort(jnp.argsort(scores, axis=1), axis=1)
        live = (placed < counts[:, None]).reshape(homes * TH).astype(jnp.int32)
        ranking = jnp.cumsum(live) - 1
        return jnp.where(live > 0, ranking % homes, -1).astype(jnp.int32)
    return jax.vmap(one_year)(jax.random.split(key, YEARS))


def levels(key, dims, pieces, least, high):
    factor_of, own = 1.0, jax.random.fold_in(key, 6)
    for position, parts in pieces:
        draws = jnp.exp(jax.random.uniform(jax.random.fold_in(own, position), (parts,), jnp.float32, least / len(pieces), high / len(pieces)))
        factor_of = factor_of * jnp.repeat(draws, dims[position] // parts).reshape([-1 if axis == position else 1 for axis in range(len(dims))])
    return factor_of


def normal_values(own_key, shape, width, reach, cuts=(), held_as=jnp.bfloat16):
    drawn = width * jax.random.normal(own_key, shape, jnp.float32)
    if cuts:
        drawn = drawn * levels(own_key, shape, cuts, -0.22, 0.18)
    return jnp.clip(drawn, -reach, reach).astype(held_as)


def setup_inputs(seed: int = 0) -> dict:
    splits = jax.random.split(jax.random.key(seed), 8)
    return {
        "forcing": normal_values(splits[0], (YEARS, TILES, CIN, TILE_ROWS, TILE_COLS), 1.0, 6.0, ((0, 4), (1, 32))),
        "hidden_prev": jnp.clip(jax.random.uniform(splits[1], (YEARS, TILES, HID, TILE_ROWS, TILE_COLS), jnp.float32, -0.8984375, 0.8984375) * levels(splits[1], (YEARS, TILES, HID, TILE_ROWS, TILE_COLS), ((0, 4), (1, 32)), -0.4, 0.0), -0.8984375, 0.8984375).astype(jnp.bfloat16),
        "cell_prev": normal_values(splits[2], (YEARS, TILES, HID, TILE_ROWS, TILE_COLS), 1.0, 4.0, ((0, 4), (1, 32))),
        "hidden_grad": normal_values(splits[3], (YEARS, TILES, HID, TILE_ROWS, TILE_COLS), (3.0 / (YEARS * TILES * TILE_ROWS * TILE_COLS) ** 0.5), 0.03125, ((0, 4), (1, 32))),
        "w_gates": normal_values(splits[4], (GATES, 9 * KIN), (9 * KIN) ** -0.5, 0.21875),
        "gate_bias": normal_values(splits[5], (GATES,), 1.0, 4.0, (), jnp.float32),
        "worker": draw_worker(jax.random.fold_in(splits[7], 71), 0),
    }


def tile_step(window, cell_old, out_grad, flag, w_gates, gate_bias):
    in_width, rows_pad, cols_pad = window.shape
    tile_rows = rows_pad - 2
    tile_cols = cols_pad - 2
    hidden_width = cell_old.shape[0]
    cells = tile_rows * tile_cols
    patches = jnp.concatenate([window[:, row_off:row_off + tile_rows, col_off:col_off + tile_cols].reshape(in_width, cells) for row_off in range(3) for col_off in range(3)], axis=0)
    pre = jnp.dot(w_gates, patches, preferred_element_type=jnp.float32) + gate_bias[:, None]
    pre = pre.reshape(4, hidden_width, cells)
    in_gate = jax.nn.sigmoid(pre[0])
    forget_gate = jax.nn.sigmoid(pre[1])
    out_gate = jax.nn.sigmoid(pre[2])
    candidate = jnp.tanh(pre[3])
    cell_before = cell_old.reshape(hidden_width, cells).astype(jnp.float32)
    cell_full = forget_gate * cell_before + in_gate * candidate
    squashed = jnp.tanh(cell_full)
    hidden_full = out_gate * squashed
    upstream = out_grad.reshape(hidden_width, cells).astype(jnp.float32)
    d_cell = upstream * out_gate * (1.0 - squashed * squashed)
    gate_grad = jnp.concatenate([
        d_cell * candidate * in_gate * (1.0 - in_gate),
        d_cell * cell_before * forget_gate * (1.0 - forget_gate),
        upstream * squashed * out_gate * (1.0 - out_gate),
        d_cell * in_gate * (1.0 - candidate * candidate)], axis=0)
    gate_grad = (gate_grad * flag).astype(jnp.bfloat16)
    weight_part = lax.dot_general(gate_grad, patches, (((1,), (1,)), ((), ())), preferred_element_type=jnp.float32)
    bias_part = jnp.sum(gate_grad.astype(jnp.float32), axis=1)
    hidden_new = hidden_full.astype(jnp.bfloat16).reshape(hidden_width, tile_rows, tile_cols)
    cell_new = cell_full.astype(jnp.bfloat16).reshape(hidden_width, tile_rows, tile_cols)
    return hidden_new, cell_new, weight_part, bias_part


def reference(forcing, hidden_prev, cell_prev, hidden_grad, w_gates, gate_bias, worker):
    years, tiles, in_ch, tile_rows, tile_cols = forcing.shape
    in_width = in_ch + hidden_prev.shape[2]
    homes = tiles // TH
    active_count = homes * CAP
    grad_weights = jnp.zeros(w_gates.shape, jnp.float32)
    grad_bias = jnp.zeros(gate_bias.shape, jnp.float32)
    hidden_list = []
    cell_list = []
    for year in range(years):
        joined = jnp.concatenate([forcing[year], hidden_prev[year]], axis=1)
        framed = joined.reshape(tiles // TW, TW, in_width, tile_rows, tile_cols).transpose(2, 0, 3, 1, 4)
        framed = framed.reshape(in_width, (tiles // TW) * tile_rows, TW * tile_cols)
        framed = jnp.pad(framed, ((0, 0), (1, 1), (1, 1)))
        live = worker[year] >= 0
        chosen = jnp.nonzero(live, size=active_count)[0].astype(jnp.int32)
        cell_year = cell_prev[year]
        grad_year = hidden_grad[year]

        def one_tile(carry, tile_id):
            row_start = (tile_id // TW) * tile_rows
            col_start = (tile_id % TW) * tile_cols
            window = lax.dynamic_slice(framed, (jnp.int32(0), row_start.astype(jnp.int32), col_start.astype(jnp.int32)), (in_width, tile_rows + 2, tile_cols + 2))
            hidden_new, cell_new, weight_part, bias_part = tile_step(window, cell_year[tile_id], grad_year[tile_id], jnp.float32(1.0), w_gates, gate_bias)
            return (carry[0] + weight_part, carry[1] + bias_part), (hidden_new, cell_new)

        (grad_weights, grad_bias), (hidden_done, cell_done) = lax.scan(one_tile, (grad_weights, grad_bias), chosen)
        hidden_list.append(hidden_prev[year].at[chosen].set(hidden_done))
        cell_list.append(cell_prev[year].at[chosen].set(cell_done))
    return jnp.stack(hidden_list), jnp.stack(cell_list), grad_weights, grad_bias
```

```python
import functools

import jax
import jax.numpy as jnp
from jax import lax
from jax.experimental import pallas as pl
from jax.experimental.pallas import tpu as pltpu
from jax.sharding import PartitionSpec as P

CIN = 16
HID = 64
KIN = CIN + HID
GATES = 4 * HID
ROWS = 8
COLS = 128
TW = 4
BAND = 4
WIDE = 3 * KIN
TAPS = 3 * WIDE
DEEP = 768
TALL = TAPS + 16

F32 = jnp.float32
BF16 = jnp.bfloat16


def load_rows(stage, tile, row, count):
    return stage[tile, pl.ds(row, count, stride=ROWS), :]


def build_row(patch_ref, line, pieces, lane):
    zero = jnp.zeros((KIN, COLS), F32)
    right = [pltpu.roll(piece, 1, 1) for piece in pieces]
    left = [pltpu.roll(piece, COLS - 1, 1) for piece in pieces]
    for tile in range(TW):
        before = right[tile - 1] if tile else zero
        after = left[tile + 1] if tile < TW - 1 else zero
        shifted = (
            jnp.where(lane == 0, before, right[tile]),
            pieces[tile],
            jnp.where(lane == COLS - 1, after, left[tile]),
        )
        span = slice(tile * COLS, (tile + 1) * COLS)
        for offset, value in enumerate(shifted):
            patch_ref[pl.ds(line * WIDE + offset * KIN, KIN), span] = value.astype(BF16)


def compute_kernel(
    first, step, last,
    worker_ref, forcing_ref, hidden_ref, cell_ref, grad_ref, above_ref, below_ref, weight_ref, bias_ref,
    *rest,
):
    if last:
        acc_in_ref, _, _, hidden_out, cell_out, sum_out = rest[:6]
        scratch = rest[6:]
    else:
        hidden_out, cell_out, sum_out = rest[:3]
        scratch = rest[3:]
    patch_ref, joined_ref, before_ref, up_ref, hidden_new, cell_new, w_ref, bias_b, total_ref = scratch
    part = pl.program_id(0)
    home = lax.axis_index("space")
    band_row = first + part * step
    base = home * (BAND * TW) + band_row * TW

    @pl.when(part == 0)
    def _():
        w_ref[...] = jnp.zeros((GATES, DEEP), BF16)
        scale = jnp.where(lax.broadcasted_iota(jnp.int32, (GATES, 1), 0) < 3 * HID, 0.5, 1.0).astype(F32)
        w_ref[:, :TAPS] = (weight_ref[...].astype(F32).T * scale).astype(BF16)
        bias_b[...] = jnp.broadcast_to(bias_ref[...] * scale, (GATES, COLS))
        patch_ref[(ROWS + 2) * WIDE :, :] = jnp.zeros((DEEP - TAPS, TW * COLS), BF16)
        if last:
            total_ref[...] = acc_in_ref[...]
        else:
            total_ref[...] = jnp.zeros_like(total_ref)

    lane = lax.broadcasted_iota(jnp.int32, (KIN, COLS), 1)
    for tile in range(TW):
        joined_ref[tile, : CIN * ROWS, :] = forcing_ref[tile].astype(F32).reshape(CIN * ROWS, COLS)
        joined_ref[tile, CIN * ROWS :, :] = hidden_ref[tile].astype(F32).reshape(HID * ROWS, COLS)
        before_ref[tile] = cell_ref[tile].astype(F32).reshape(HID * ROWS, COLS)
        live = worker_ref[base + tile] >= 0
        up = grad_ref[tile].astype(F32).reshape(HID * ROWS, COLS)
        up_ref[tile] = jnp.where(live, up, 0.0)

    build_row(patch_ref, 0, [above_ref[0, tile].astype(F32) for tile in range(TW)], lane)
    build_row(patch_ref, ROWS + 1, [below_ref[0, tile].astype(F32) for tile in range(TW)], lane)
    for row in range(ROWS):
        build_row(patch_ref, row + 1, [load_rows(joined_ref, tile, row, KIN) for tile in range(TW)], lane)

    ones = jnp.ones((TALL - TAPS, TW * COLS), BF16)

    def one_row(row, carry):
        at = pl.multiple_of(row * WIDE, 16)
        pre = jnp.dot(w_ref[...], patch_ref[pl.ds(at, DEEP), :], preferred_element_type=F32)
        grads = []
        for tile in range(TW):
            span = slice(tile * COLS, (tile + 1) * COLS)
            blocks = [
                jnp.tanh(pre[k * HID : (k + 1) * HID, span] + bias_b[k * HID : (k + 1) * HID, :]) for k in range(4)
            ]
            in_gate, forget_gate, out_gate = [0.5 * block + 0.5 for block in blocks[:3]]
            candidate = blocks[3]
            cell_before = load_rows(before_ref, tile, row, HID)
            upstream = load_rows(up_ref, tile, row, HID)
            cell_full = forget_gate * cell_before + in_gate * candidate
            squashed = jnp.tanh(cell_full)
            hidden_new[tile, pl.ds(row, HID, stride=ROWS), :] = out_gate * squashed
            cell_new[tile, pl.ds(row, HID, stride=ROWS), :] = cell_full
            raised = upstream * out_gate
            d_cell = raised * (1.0 - squashed * squashed)
            d_in = d_cell * in_gate
            grads.append(
                jnp.concatenate(
                    [
                        d_in * candidate * (1.0 - in_gate),
                        d_cell * cell_before * forget_gate * (1.0 - forget_gate),
                        raised * squashed * (1.0 - out_gate),
                        d_in * (1.0 - candidate * candidate),
                    ],
                    axis=0,
                ).astype(BF16)
            )
        gate_grad = jnp.concatenate(grads, axis=1)
        left = jnp.concatenate([patch_ref[pl.ds(at, TAPS), :], ones], axis=0)
        total_ref[...] += lax.dot_general(
            left, gate_grad, (((1,), (1,)), ((), ())), preferred_element_type=F32
        )
        return carry

    lax.fori_loop(0, ROWS, one_row, 0)

    for tile in range(TW):
        live = worker_ref[base + tile] >= 0
        fresh = hidden_new[tile].reshape(HID, ROWS, COLS).astype(BF16)
        hidden_out[tile] = jnp.where(live, fresh, hidden_ref[tile])
        fresh = cell_new[tile].reshape(HID, ROWS, COLS).astype(BF16)
        cell_out[tile] = jnp.where(live, fresh, cell_ref[tile])

    @pl.when(part == 1)
    def _():
        if last:
            sum_out[:, :TALL] = total_ref[...].T.astype(BF16)
            sum_out[:, TALL:] = jnp.zeros((GATES, DEEP - TALL), BF16)
        else:
            sum_out[...] = total_ref[...]


def compute(first, step, worker, forcing, hidden, cell, grad, above, below, weight, bias, carried=None):
    last = carried is not None

    def block(channels):
        return pl.BlockSpec((TW, channels, ROWS, COLS), lambda part, _: (first + part * step, 0, 0, 0))

    edge = pl.BlockSpec((1, TW, KIN, COLS), lambda part, _: (part, 0, 0, 0))

    def whole(*shape):
        return pl.BlockSpec(shape, lambda part, _: (0,) * len(shape), pipeline_mode=pl.Buffered(1))

    in_specs = [block(CIN), block(HID), block(HID), block(HID), edge, edge, whole(TAPS, GATES), whole(GATES, 1)]
    operands = [worker, forcing, hidden, cell, grad, above, below, weight, bias]
    aliases = {}
    if last:
        in_specs += [whole(TALL, GATES), pl.BlockSpec(memory_space=pl.ANY), pl.BlockSpec(memory_space=pl.ANY)]
        aliases = {len(operands) + 1: 0, len(operands) + 2: 1}
        operands += list(carried)
        sum_shape = jax.ShapeDtypeStruct((GATES, DEEP), BF16)
    else:
        sum_shape = jax.ShapeDtypeStruct((TALL, GATES), F32)
    state = jax.ShapeDtypeStruct(hidden.shape, BF16)
    stage = pltpu.VMEM((TW, HID * ROWS, COLS), F32)
    return pl.pallas_call(
        functools.partial(compute_kernel, first, step, last),
        grid_spec=pltpu.PrefetchScalarGridSpec(
            num_scalar_prefetch=1,
            grid=(2,),
            in_specs=in_specs,
            out_specs=[block(HID), block(HID), whole(*sum_shape.shape)],
            scratch_shapes=[
                pltpu.VMEM(((ROWS + 2) * WIDE + DEEP - TAPS, TW * COLS), BF16),
                pltpu.VMEM((TW, KIN * ROWS, COLS), F32),
                stage, stage, stage, stage,
                pltpu.VMEM((GATES, DEEP), BF16),
                pltpu.VMEM((GATES, COLS), F32),
                pltpu.VMEM((TALL, GATES), F32),
            ],
        ),
        out_shape=[state, state, sum_shape],
        input_output_aliases=aliases,
        compiler_params=pltpu.CompilerParams(vmem_limit_bytes=40 << 20),
        cost_estimate=pl.CostEstimate(
            flops=8 * TW * ROWS * COLS * TAPS * GATES, bytes_accessed=6 << 20, transcendentals=0
        ),
        name="second" if last else "first",
    )(*operands)


def shards(forcing, hidden_prev, cell_prev, hidden_grad, w_gates, gate_bias, worker):
    size = lax.axis_size("space")
    forcing, hidden, cell, grad = forcing[0], hidden_prev[0], cell_prev[0], hidden_grad[0]
    joined_f = forcing.reshape(BAND, TW, CIN, ROWS, COLS)
    joined_h = hidden.reshape(BAND, TW, HID, ROWS, COLS)
    leading = jnp.concatenate([joined_f[:, :, :, 0], joined_h[:, :, :, 0]], axis=2)
    ending = jnp.concatenate([joined_f[:, :, :, ROWS - 1], joined_h[:, :, :, ROWS - 1]], axis=2)
    up = [(i, i + 1) for i in range(size - 1)]
    down = [(j, i) for i, j in up]
    before = lax.ppermute(ending[BAND - 1 :], "space", up)
    after = lax.ppermute(leading[:1], "space", down)
    weight = w_gates.T
    bias = gate_bias[:, None]
    tiles = worker[0]
    carried = compute(
        1, 1, tiles, forcing, hidden, cell, grad, ending[0:2], leading[2:4], weight, bias
    )
    above = jnp.concatenate([before, ending[2:3]], axis=0)
    below = jnp.concatenate([leading[1:2], after], axis=0)
    hidden_next, cell_next, part = compute(
        0, 3, tiles, forcing, hidden, cell, grad, above, below, weight, bias,
        carried=(carried[2], carried[0], carried[1]),
    )
    share = GATES // size
    pieces = lax.all_to_all(part.reshape(size, share, DEEP), "space", 0, 0, tiled=True)
    mine = jnp.sum(pieces.astype(F32), axis=0).astype(BF16)
    years = lax.axis_size("dp")
    total = mine.astype(F32)
    for k in range(1, years):
        other = lax.ppermute(mine, "dp", [(i, (i + k) % years) for i in range(years)])
        total = total + other.astype(F32)
    return hidden_next[None], cell_next[None], total[:, :TAPS], total[:, TAPS]


def solution(mesh):
    tiles = P("dp", "space", None, None, None)
    return jax.shard_map(
        shards,
        mesh=mesh,
        in_specs=(tiles, tiles, tiles, tiles, P(), P(), P("dp", None)),
        out_specs=(tiles, tiles, P("space", None), P("space")),
        check_vma=False,
    )
```

```python
import functools

import jax
import jax.numpy as jnp
from jax import lax
from jax.experimental import pallas as pl
from jax.experimental.pallas import tpu as pltpu
from jax.sharding import PartitionSpec as P

CIN = 16
HID = 64
KIN = CIN + HID
GATES = 4 * HID
ROWS = 8
COLS = 128
TW = 4
BAND = 4
WIDE = 3 * KIN
LINE = 256
CHUNK = 16
TAPS = 3 * WIDE
DEEP = 3 * LINE
ROW = TW * COLS

F32 = jnp.float32
BF16 = jnp.bfloat16


def load_rows(stage, tile, row, count, start=0):
    return stage[tile, pl.ds(row + start * ROWS, count, stride=ROWS), :]


def build_row(patch_ref, line, pieces, lane):
    zero = jnp.zeros((KIN, COLS), F32)
    right = [pltpu.roll(piece, 1, 1) for piece in pieces]
    left = [pltpu.roll(piece, COLS - 1, 1) for piece in pieces]
    for tile in range(TW):
        before = right[tile - 1] if tile else zero
        after = left[tile + 1] if tile < TW - 1 else zero
        shifted = (
            jnp.where(lane == 0, before, right[tile]),
            pieces[tile],
            jnp.where(lane == COLS - 1, after, left[tile]),
        )
        span = slice(tile * COLS, (tile + 1) * COLS)
        for offset, value in enumerate(shifted):
            patch_ref[line * LINE + offset * KIN : line * LINE + (offset + 1) * KIN, span] = value.astype(BF16)


def edge_kernel(*refs):
    forcing_refs, hidden_refs = refs[:3], refs[3:6]
    near_ref, far_ref, ending_0, leading_2, ending_2, leading_3 = refs[6:12]
    joined_ref = refs[12]
    odd = lax.rem(lax.axis_index("space"), 2) == 1
    for tile in range(TW):
        for which in range(3):
            slot = which * TW + tile
            joined_ref[slot, : CIN * ROWS, :] = forcing_refs[which][tile].astype(F32).reshape(CIN * ROWS, COLS)
            joined_ref[slot, CIN * ROWS :, :] = hidden_refs[which][tile].astype(F32).reshape(HID * ROWS, COLS)
        first_row = load_rows(joined_ref, tile, 0, KIN)
        last_row = load_rows(joined_ref, 2 * TW + tile, ROWS - 1, KIN)
        near_ref[tile] = jnp.where(odd, first_row, last_row).astype(BF16)
        far_ref[tile] = jnp.where(odd, last_row, first_row).astype(BF16)
        ending_0[tile] = load_rows(joined_ref, tile, ROWS - 1, KIN).astype(BF16)
        leading_2[tile] = load_rows(joined_ref, TW + tile, 0, KIN).astype(BF16)
        ending_2[tile] = load_rows(joined_ref, TW + tile, ROWS - 1, KIN).astype(BF16)
        leading_3[tile] = load_rows(joined_ref, 2 * TW + tile, 0, KIN).astype(BF16)


def edges(forcing, hidden):
    def block(channels, band_row):
        return pl.BlockSpec((TW, channels, ROWS, COLS), lambda part: (band_row, 0, 0, 0))

    shape = jax.ShapeDtypeStruct((TW, KIN, COLS), BF16)
    picked = (0, 2, 3)
    return pl.pallas_call(
        edge_kernel,
        grid=(1,),
        in_specs=[block(CIN, i) for i in picked] + [block(HID, i) for i in picked],
        out_specs=[pl.BlockSpec(memory_space=pltpu.VMEM)] * 6,
        out_shape=[shape] * 6,
        scratch_shapes=[pltpu.VMEM((3 * TW, KIN * ROWS, COLS), F32)],
        compiler_params=pltpu.CompilerParams(vmem_limit_bytes=24 << 20),
        cost_estimate=pl.CostEstimate(flops=0, bytes_accessed=3 << 20, transcendentals=0),
        name="edges",
    )(forcing, forcing, forcing, hidden, hidden, hidden)


def prepare(weight_ref, bias_ref, w_ref, patch_ref, wide_ref):
    wide_ref[...] = jnp.zeros((DEEP, GATES), F32)
    for tap in range(3):
        wide_ref[tap * LINE : tap * LINE + WIDE, :] = weight_ref[tap * WIDE : (tap + 1) * WIDE, :].astype(F32)
    rest = bias_ref[...]
    for piece in range(3):
        value = rest.astype(BF16).astype(F32)
        wide_ref[WIDE + piece : WIDE + piece + 1, :] = value
        rest = rest - value
    gate = lax.broadcasted_iota(jnp.int32, (GATES, 1), 0)
    w_ref[...] = (wide_ref[...].T * jnp.where(gate < 3 * HID, 0.5, 1.0)).astype(BF16)


def fill_ones(patch_ref):
    index = lax.broadcasted_iota(jnp.int32, (LINE - WIDE, ROW), 0)
    ones = jnp.where(index < 3, 1.0, 0.0).astype(BF16)
    for line in range(ROWS + 2):
        patch_ref[line * LINE + WIDE : (line + 1) * LINE, :] = ones


def gates_of_row(pre_ref, before_ref, up_ref, hidden_new, cell_new, grad_ref, row):
    for tile in range(TW):
        span = slice(tile * COLS, (tile + 1) * COLS)
        out_span = slice(row * ROW + tile * COLS, row * ROW + (tile + 1) * COLS)
        for start in range(0, HID, CHUNK):
            in_half, forget_half, out_half, candidate = [
                jnp.tanh(pre_ref[k * HID + start : k * HID + start + CHUNK, span]) for k in range(4)
            ]
            in_gate, forget_gate, out_gate = [0.5 * half + 0.5 for half in (in_half, forget_half, out_half)]
            cell_before = load_rows(before_ref, tile, row, CHUNK, start)
            upstream = load_rows(up_ref, tile, row, CHUNK, start)
            kept = forget_gate * cell_before
            cell_full = kept + in_gate * candidate
            squashed = jnp.tanh(cell_full)
            place = pl.ds(row + start * ROWS, CHUNK, stride=ROWS)
            hidden_new[tile, place, :] = out_gate * squashed
            cell_new[tile, place, :] = cell_full
            raised = upstream * out_gate
            d_cell = raised * (1.0 - squashed * squashed)
            d_in = d_cell * in_gate
            parts = [
                d_in * candidate * (1.0 - in_gate),
                d_cell * kept * (1.0 - forget_gate),
                raised * squashed * (1.0 - out_gate),
                d_in * (1.0 - candidate * candidate),
            ]
            for k, part in enumerate(parts):
                grad_ref[k * HID + start : k * HID + start + CHUNK, out_span] = part.astype(BF16)


def compute_kernel(
    first, step, last,
    worker_ref,
    *rest,
):
    if last:
        (forcing_buf, hidden_buf, cell_buf, grad_buf, near_halo, leading_1, ending_2, far_halo,
         w_ref, acc_in_ref, _, _, hidden_hbm_out, cell_hbm_out, own_out, other_out) = rest[:16]
        scratch = rest[16:]
    else:
        sources = rest[:4]
        (ending_0, leading_2, leading_3, weight_ref, bias_ref,
         hidden_hbm_out, cell_hbm_out, sum_out, w_ref, leading_1) = rest[4:14]
        ahead = rest[14:18]
        buffers, (in_sem, ahead_sem), scratch = rest[18:22], rest[22:24], rest[24:]
        forcing_buf, hidden_buf, cell_buf, grad_buf = buffers
    (hidden_res, cell_res, out_sem,
     patch_ref, joined_ref, before_ref, up_ref, hidden_new, cell_new,
     pre_a, pre_b, grad_ref, total_ref) = scratch
    part = pl.program_id(0)
    home = lax.axis_index("space")
    base = home * (BAND * TW) + (first + part * step) * TW

    def fetch(which, index):
        return pltpu.make_async_copy(
            sources[which].at[pl.ds((first + index * step) * TW, TW)], buffers[which].at[index], in_sem.at[which, index]
        )

    def fetch_ahead(which, index):
        return pltpu.make_async_copy(
            sources[which].at[pl.ds(index * (BAND - 1) * TW, TW)], ahead[which].at[index], ahead_sem.at[which, index]
        )

    def flush(which, index):
        hbm, buf = ((hidden_hbm_out, hidden_res), (cell_hbm_out, cell_res))[which]
        return pltpu.make_async_copy(
            buf.at[index], hbm.at[pl.ds((first + index * step) * TW, TW)], out_sem.at[which, index]
        )

    @pl.when(part == 0)
    def _():
        if not last:
            for which in range(4):
                fetch(which, 0).start()
        fill_ones(patch_ref)
        if last:
            total_ref[...] = acc_in_ref[...]
        else:
            prepare(weight_ref, bias_ref, w_ref, patch_ref, total_ref)
            total_ref[...] = jnp.zeros_like(total_ref)

    if not last:
        @pl.when(part == 1)
        def _():
            patch_ref[:WIDE, :] = patch_ref[ROWS * LINE : ROWS * LINE + WIDE, :]

    if not last:
        fetch(0, part).wait()
        fetch(1, part).wait()
    lane = lax.broadcasted_iota(jnp.int32, (KIN, COLS), 1)
    for tile in range(TW):
        joined_ref[tile, : CIN * ROWS, :] = forcing_buf[part, tile].astype(F32).reshape(CIN * ROWS, COLS)
        joined_ref[tile, CIN * ROWS :, :] = hidden_buf[part, tile].astype(F32).reshape(HID * ROWS, COLS)
    if last:
        odd = lax.rem(home, 2) == 1
        near = [near_halo[t].astype(F32) for t in range(TW)]
        far = [far_halo[t].astype(F32) for t in range(TW)]
        above = [
            jnp.where(part == 0, jnp.where(odd, near[t], far[t]), ending_2[t].astype(F32)) for t in range(TW)
        ]
        below = [
            jnp.where(part == 0, leading_1[t].astype(F32), jnp.where(odd, far[t], near[t])) for t in range(TW)
        ]
        build_row(patch_ref, 0, above, lane)
    else:
        below = [jnp.where(part == 0, leading_2[t].astype(F32), leading_3[t].astype(F32)) for t in range(TW)]

        @pl.when(part == 0)
        def _():
            build_row(patch_ref, 0, [ending_0[t].astype(F32) for t in range(TW)], lane)
            for tile in range(TW):
                leading_1[tile] = load_rows(joined_ref, tile, 0, KIN).astype(BF16)

    if not last:
        fetch(2, part).wait()
        fetch(3, part).wait()

        @pl.when(part == 0)
        def _():
            for which in range(4):
                fetch(which, 1).start()

        @pl.when(part == 1)
        def _():
            for index in range(2):
                for which in range(4):
                    fetch_ahead(which, index).start()


    def build(line):
        if line == ROWS + 1:
            pieces = below
        else:
            pieces = [load_rows(joined_ref, tile, line - 1, KIN) for tile in range(TW)]
        build_row(patch_ref, line, pieces, lane)

    pres = (pre_a, pre_b)

    def forward(row):
        pres[row % 2][...] = jnp.dot(
            w_ref[...], patch_ref[row * LINE : row * LINE + DEEP, :], preferred_element_type=F32
        )

    def backward():
        left = jnp.concatenate([patch_ref[row * LINE : row * LINE + DEEP, :] for row in range(ROWS)], axis=1)
        total_ref[...] += lax.dot_general(
            left, grad_ref[...], (((1,), (1,)), ((), ())), preferred_element_type=F32
        )

    for line in range(1, 3):
        build(line)
    forward(0)
    for tile in range(TW):
        before_ref[tile] = cell_buf[part, tile].astype(F32).reshape(HID * ROWS, COLS)
        live = worker_ref[base + tile] >= 0
        up = grad_buf[part, tile].astype(F32).reshape(HID * ROWS, COLS)
        up_ref[tile] = jnp.where(live, up, 0.0)
    for row in range(ROWS):
        if row + 1 < ROWS:
            build(row + 3)
            forward(row + 1)
        gates_of_row(pres[row % 2], before_ref, up_ref, hidden_new, cell_new, grad_ref, row)

    for tile in range(TW):
        live = worker_ref[base + tile] >= 0
        fresh = hidden_new[tile].reshape(HID, ROWS, COLS).astype(BF16)
        hidden_res[part, tile] = jnp.where(live, fresh, hidden_buf[part, tile])
        fresh = cell_new[tile].reshape(HID, ROWS, COLS).astype(BF16)
        cell_res[part, tile] = jnp.where(live, fresh, cell_buf[part, tile])
    flush(0, part).start()
    flush(1, part).start()
    backward()

    @pl.when(part == 1)
    def _():
        if last:
            packed = jnp.concatenate(
                [total_ref[tap * LINE : tap * LINE + WIDE, :] for tap in range(3)]
                + [total_ref[WIDE:LINE, :], jnp.zeros((DEEP - TAPS - LINE + WIDE, GATES), F32)],
                axis=0,
            )
            turned = packed.T
            odd = lax.rem(home, 2) == 1
            for pair in range(GATES // (2 * ROWS)):
                even_half = turned[2 * pair * ROWS : (2 * pair + 1) * ROWS]
                odd_half = turned[(2 * pair + 1) * ROWS : (2 * pair + 2) * ROWS]
                own_out[pair] = jnp.where(odd, odd_half, even_half)
                other_out[pair] = jnp.where(odd, even_half, odd_half).astype(BF16)
        else:
            sum_out[...] = total_ref[...]
            for index in range(2):
                for which in range(4):
                    fetch_ahead(which, index).wait()
        for index in range(2):
            for which in range(2):
                flush(which, index).wait()


def compute(first, step, worker, carried, hidden, last):
    resident = pl.BlockSpec(memory_space=pltpu.VMEM)
    anywhere = pl.BlockSpec(memory_space=pl.ANY)
    operands = [worker] + carried
    state = jax.ShapeDtypeStruct(hidden.shape, BF16)
    small = (2, TW, CIN, ROWS, COLS)
    large = (2, TW, HID, ROWS, COLS)
    out_shape = [state, state]
    aliases = {}
    scratch = []
    if last:
        in_specs = [resident] * 10 + [anywhere] * 2
        aliases = {11: 0, 12: 1}
        out_shape.append(jax.ShapeDtypeStruct((GATES // (2 * ROWS), ROWS, DEEP), F32))
        out_shape.append(jax.ShapeDtypeStruct((GATES // (2 * ROWS), ROWS, DEEP), BF16))
    else:
        in_specs = [anywhere] * 4 + [resident] * 5
        out_shape.append(jax.ShapeDtypeStruct((DEEP, GATES), F32))
        out_shape.append(jax.ShapeDtypeStruct((GATES, DEEP), BF16))
        out_shape.append(jax.ShapeDtypeStruct((TW, KIN, COLS), BF16))
        out_shape += [jax.ShapeDtypeStruct(shape, BF16) for shape in (small, large, large, large)]
        scratch = [pltpu.VMEM(shape, BF16) for shape in (small, large, large, large)]
        scratch += [pltpu.SemaphoreType.DMA((4, 2)), pltpu.SemaphoreType.DMA((4, 2))]
    stage = pltpu.VMEM((TW, HID * ROWS, COLS), F32)
    return pl.pallas_call(
        functools.partial(compute_kernel, first, step, last),
        grid_spec=pltpu.PrefetchScalarGridSpec(
            num_scalar_prefetch=1,
            grid=(2,),
            in_specs=in_specs,
            out_specs=[anywhere, anywhere] + [resident] * (len(out_shape) - 2),
            scratch_shapes=scratch + [
                pltpu.VMEM(large, BF16),
                pltpu.VMEM(large, BF16),
                pltpu.SemaphoreType.DMA((2, 2)),
                pltpu.VMEM(((ROWS + 2) * LINE, ROW), BF16),
                pltpu.VMEM((TW, KIN * ROWS, COLS), F32),
                stage, stage, stage, stage,
                pltpu.VMEM((GATES, ROW), F32),
                pltpu.VMEM((GATES, ROW), F32),
                pltpu.VMEM((GATES, ROWS * ROW), BF16),
                pltpu.VMEM((DEEP, GATES), F32),
            ],
        ),
        out_shape=out_shape,
        input_output_aliases=aliases,
        compiler_params=pltpu.CompilerParams(vmem_limit_bytes=40 << 20),
        cost_estimate=pl.CostEstimate(
            flops=8 * TW * ROWS * COLS * TAPS * GATES, bytes_accessed=6 << 20, transcendentals=0
        ),
        name="second" if last else "first",
    )(*operands)


def shards(forcing, hidden_prev, cell_prev, hidden_grad, w_gates, gate_bias, worker):
    size = lax.axis_size("space")
    forcing, hidden, cell, grad = [
        pltpu.with_memory_space_constraint(array[0], pltpu.HBM)
        for array in (forcing, hidden_prev, cell_prev, hidden_grad)
    ]
    near, far, ending_0, leading_2, ending_2, leading_3 = edges(forcing, hidden)
    near_halo = lax.ppermute(near, "space", [(i, i ^ 1) for i in range(size)])
    far_pairs = [(i, i + 1) for i in range(1, size - 1, 2)]
    far_halo = lax.ppermute(far, "space", far_pairs + [(j, i) for i, j in far_pairs])
    tiles = worker[0]
    hidden_part, cell_part, total, w, leading_1, *ahead = compute(
        1, 1, tiles,
        [forcing, hidden, cell, grad, ending_0, leading_2, leading_3, w_gates.T, gate_bias[None, :]], hidden, False,
    )
    hidden_next, cell_next, own, other = compute(
        0, 3, tiles,
        [*ahead, near_halo, leading_1, ending_2, far_halo, w, total, hidden_part, cell_part], hidden, True,
    )
    half = own + lax.ppermute(other, "space", [(i, i ^ 1) for i in range(size)]).astype(F32)
    groups = [list(range(core, size, 2)) for core in range(2)]
    pieces = lax.all_to_all(half.astype(BF16), "space", 0, 0, tiled=True, axis_index_groups=groups)
    mine = jnp.sum(pieces.astype(F32), axis=0).astype(BF16)
    years = lax.axis_size("dp")
    total = mine.astype(F32)
    for k in range(1, years):
        other = lax.ppermute(mine, "dp", [(i, (i + k) % years) for i in range(years)])
        total = total + other.astype(F32)
    return hidden_next[None], cell_next[None], total[:, :TAPS], total[:, TAPS]


def solution(mesh):
    tiles = P("dp", "space", None, None, None)
    return jax.shard_map(
        shards,
        mesh=mesh,
        in_specs=(tiles, tiles, tiles, tiles, P(), P(), P("dp", None)),
        out_specs=(tiles, tiles, P("space", None), P("space")),
        check_vma=False,
    )
```

```python
import functools

import jax
import jax.numpy as jnp
from jax import lax
from jax.experimental import pallas as pl
from jax.experimental.pallas import tpu as pltpu
from jax.sharding import PartitionSpec as P

CIN = 16
HID = 64
KIN = CIN + HID
GATES = 4 * HID
ROWS = 8
COLS = 128
TW = 4
BAND = 4
WIDE = 3 * KIN
LINE = 256
CHUNK = 16
TAPS = 3 * WIDE
DEEP = 3 * LINE
ROW = TW * COLS

F32 = jnp.float32
BF16 = jnp.bfloat16


def load_rows(stage, tile, row, count, start=0):
    return stage[tile, pl.ds(row + start * ROWS, count, stride=ROWS), :]


def build_row(patch_ref, line, pieces, lane):
    zero = jnp.zeros((KIN, COLS), F32)
    right = [pltpu.roll(piece, 1, 1) for piece in pieces]
    left = [pltpu.roll(piece, COLS - 1, 1) for piece in pieces]
    for tile in range(TW):
        before = right[tile - 1] if tile else zero
        after = left[tile + 1] if tile < TW - 1 else zero
        shifted = (
            jnp.where(lane == 0, before, right[tile]),
            pieces[tile],
            jnp.where(lane == COLS - 1, after, left[tile]),
        )
        span = slice(tile * COLS, (tile + 1) * COLS)
        for offset, value in enumerate(shifted):
            patch_ref[line * LINE + offset * KIN : line * LINE + (offset + 1) * KIN, span] = value.astype(BF16)


def edge_kernel(forcing_hbm, hidden_hbm, near_ref, far_ref, ending_0, leading_3, forcing_buf, hidden_buf, joined_ref, sem):
    odd = lax.rem(lax.axis_index("space"), 2) == 1
    copies = []
    for slot, band_row in ((0, 0), (2, BAND - 1), (1, 1)):
        for which, (hbm, buf) in enumerate(((forcing_hbm, forcing_buf), (hidden_hbm, hidden_buf))):
            copies.append(
                pltpu.make_async_copy(hbm.at[pl.ds(band_row * TW, TW)], buf.at[slot], sem.at[which, slot])
            )
            copies[-1].start()
    for copy in copies[:4]:
        copy.wait()
    for tile in range(TW):
        for which in range(2):
            slot = which * TW + tile
            joined_ref[slot, : CIN * ROWS, :] = forcing_buf[2 * which, tile].astype(F32).reshape(CIN * ROWS, COLS)
            joined_ref[slot, CIN * ROWS :, :] = hidden_buf[2 * which, tile].astype(F32).reshape(HID * ROWS, COLS)
        first_row = load_rows(joined_ref, tile, 0, KIN)
        last_row = load_rows(joined_ref, TW + tile, ROWS - 1, KIN)
        near_ref[tile] = jnp.where(odd, first_row, last_row).astype(BF16)
        far_ref[tile] = jnp.where(odd, last_row, first_row).astype(BF16)
        ending_0[tile] = load_rows(joined_ref, tile, ROWS - 1, KIN).astype(BF16)
        leading_3[tile] = load_rows(joined_ref, TW + tile, 0, KIN).astype(BF16)
    for copy in copies[4:]:
        copy.wait()


def edges(forcing, hidden):
    shape = jax.ShapeDtypeStruct((TW, KIN, COLS), BF16)
    return pl.pallas_call(
        edge_kernel,
        in_specs=[pl.BlockSpec(memory_space=pl.ANY)] * 2,
        out_specs=[pl.BlockSpec(memory_space=pltpu.VMEM)] * 6,
        out_shape=[shape] * 4 + [jax.ShapeDtypeStruct((3, TW, n, ROWS, COLS), BF16) for n in (CIN, HID)],
        scratch_shapes=[pltpu.VMEM((2 * TW, KIN * ROWS, COLS), F32), pltpu.SemaphoreType.DMA((2, 3))],
        compiler_params=pltpu.CompilerParams(vmem_limit_bytes=24 << 20),
        cost_estimate=pl.CostEstimate(flops=0, bytes_accessed=3 << 20, transcendentals=0),
        name="edges",
    )(forcing, hidden)


def prepare(weight_ref, bias_ref, w_ref, wide_ref):
    wide_ref[...] = jnp.zeros((DEEP, GATES), F32)
    for tap in range(3):
        wide_ref[tap * LINE : tap * LINE + WIDE, :] = weight_ref[tap * WIDE : (tap + 1) * WIDE, :].astype(F32)
    rest = bias_ref[...]
    for piece in range(3):
        value = rest.astype(BF16).astype(F32)
        wide_ref[WIDE + piece : WIDE + piece + 1, :] = value
        rest = rest - value
    gate = lax.broadcasted_iota(jnp.int32, (GATES, 1), 0)
    w_ref[...] = (wide_ref[...].T * jnp.where(gate < 3 * HID, 0.5, 1.0)).astype(BF16)


def fill_ones(patch_ref):
    index = lax.broadcasted_iota(jnp.int32, (LINE - WIDE, ROW), 0)
    ones = jnp.where(index < 3, 1.0, 0.0).astype(BF16)
    for line in range(ROWS + 2):
        patch_ref[line * LINE + WIDE : (line + 1) * LINE, :] = ones


def gates_of_row(pre_ref, before_ref, up_ref, hidden_new, cell_new, grad_ref, row):
    for tile in range(TW):
        span = slice(tile * COLS, (tile + 1) * COLS)
        out_span = slice(row * ROW + tile * COLS, row * ROW + (tile + 1) * COLS)
        for start in range(0, HID, CHUNK):
            in_half, forget_half, out_half, candidate = [
                jnp.tanh(pre_ref[k * HID + start : k * HID + start + CHUNK, span]) for k in range(4)
            ]
            in_gate, forget_gate, out_gate = [0.5 * half + 0.5 for half in (in_half, forget_half, out_half)]
            cell_before = load_rows(before_ref, tile, row, CHUNK, start)
            upstream = load_rows(up_ref, tile, row, CHUNK, start)
            kept = forget_gate * cell_before
            cell_full = kept + in_gate * candidate
            squashed = jnp.tanh(cell_full)
            place = pl.ds(row + start * ROWS, CHUNK, stride=ROWS)
            hidden_new[tile, place, :] = out_gate * squashed
            cell_new[tile, place, :] = cell_full
            raised = upstream * out_gate
            d_cell = raised * (1.0 - squashed * squashed)
            d_in = d_cell * in_gate
            parts = [
                d_in * candidate * (1.0 - in_gate),
                d_cell * kept * (1.0 - forget_gate),
                raised * squashed * (1.0 - out_gate),
                d_in * (1.0 - candidate * candidate),
            ]
            for k, part in enumerate(parts):
                grad_ref[k * HID + start : k * HID + start + CHUNK, out_span] = part.astype(BF16)


def compute_kernel(
    first, step, last,
    worker_ref,
    *rest,
):
    if last:
        (forcing_in, hidden_in, cell_buf, grad_buf, near_halo, leading_1, ending_2, far_halo,
         w_ref, acc_in_ref, _, _, hidden_hbm_out, cell_hbm_out, own_out, other_out) = rest[:16]
        scratch = rest[16:]
        state_of = [(forcing_in.at[2 * part], hidden_in.at[2 * part]) for part in range(2)]
    else:
        sources = rest[:4]
        (forcing_in, hidden_in, ending_0, leading_3, weight_ref, bias_ref,
         hidden_hbm_out, cell_hbm_out, sum_out, w_ref, leading_1, ending_2) = rest[4:16]
        ahead = rest[16:18]
        (forcing_own, hidden_own, cell_buf, grad_buf, in_sem, ahead_sem) = rest[18:24]
        scratch = rest[24:]
        state_of = [(forcing_in.at[1], hidden_in.at[1]), (forcing_own, hidden_own)]
    hidden_res, cell_res, out_sem, total_ref, pre_a, pre_b = scratch[:6]
    stages = scratch[6:]
    home = lax.axis_index("space")
    odd = lax.rem(home, 2) == 1
    pres = (pre_a, pre_b)

    def fetch(which, index):
        buffer = (forcing_own, hidden_own, cell_buf.at[index], grad_buf.at[index])[which]
        return pltpu.make_async_copy(
            sources[which].at[pl.ds((first + index * step) * TW, TW)], buffer, in_sem.at[which, index]
        )

    def fetch_ahead(which, index):
        return pltpu.make_async_copy(
            sources[which + 2].at[pl.ds(index * (BAND - 1) * TW, TW)], ahead[which].at[index], ahead_sem.at[which, index]
        )

    def flush(which, index):
        hbm, buf = ((hidden_hbm_out, hidden_res), (cell_hbm_out, cell_res))[which]
        return pltpu.make_async_copy(
            buf.at[index], hbm.at[pl.ds((first + index * step) * TW, TW)], out_sem.at[which, index]
        )

    def run(patches, grads):
        if not last:
            for which, index in ((2, 0), (3, 0), (0, 1), (1, 1)):
                fetch(which, index).start()
        for patch_ref in patches:
            fill_ones(patch_ref)
        if not last:
            prepare(weight_ref, bias_ref, w_ref, total_ref)
        for part in range(2):
            one_part(part, patches, grads[part], stages[0], *stages[6 * part : 6 * part + 6])
        if last:
            packed = jnp.concatenate(
                [total_ref[tap * LINE : tap * LINE + WIDE, :] for tap in range(3)]
                + [total_ref[WIDE:LINE, :], jnp.zeros((DEEP - TAPS - LINE + WIDE, GATES), F32)],
                axis=0,
            )
            turned = packed.T
            for pair in range(GATES // (2 * ROWS)):
                even_half = turned[2 * pair * ROWS : (2 * pair + 1) * ROWS]
                odd_half = turned[(2 * pair + 1) * ROWS : (2 * pair + 2) * ROWS]
                own_out[pair] = jnp.where(odd, odd_half, even_half)
                other_out[pair] = jnp.where(odd, even_half, odd_half).astype(BF16)
        else:
            sum_out[...] = total_ref[...]
            for index in range(2):
                for which in range(2):
                    fetch_ahead(which, index).wait()
        for index in range(2):
            for which in range(2):
                flush(which, index).wait()

    def one_part(part, patches, grad_ref, joined_0, joined_ref, before_ref, up_ref, hidden_new, cell_new, _):
        patch_ref = patches[part]
        base = home * (BAND * TW) + (first + part * step) * TW
        forcing_buf, hidden_buf = state_of[part]
        lane = lax.broadcasted_iota(jnp.int32, (KIN, COLS), 1)

        def stage(which, into):
            forcing_ref, hidden_ref = state_of[which]
            for tile in range(TW):
                into[tile, : CIN * ROWS, :] = forcing_ref[tile].astype(F32).reshape(CIN * ROWS, COLS)
                into[tile, CIN * ROWS :, :] = hidden_ref[tile].astype(F32).reshape(HID * ROWS, COLS)

        if last or part == 0:
            stage(part, joined_ref)

        def halo(even_ref, odd_ref):
            return [jnp.where(odd, odd_ref[t].astype(F32), even_ref[t].astype(F32)) for t in range(TW)]

        def plain(ref):
            return [ref[t].astype(F32) for t in range(TW)]

        if last:
            above = plain(ending_2) if part else halo(far_halo, near_halo)
            below = halo(near_halo, far_halo) if part else plain(leading_1)
        else:
            above = None if part else plain(ending_0)
            below = plain(leading_3) if part else None
        if above is None:
            patch_ref[:WIDE, :] = patches[0][ROWS * LINE : ROWS * LINE + WIDE, :]
        else:
            build_row(patch_ref, 0, above, lane)

        def build(line):
            if line == ROWS + 1 and below is None:
                pieces = [load_rows(stages[6], tile, 0, KIN) for tile in range(TW)]
            elif line == ROWS + 1:
                pieces = below
            else:
                pieces = [load_rows(joined_ref, tile, line - 1, KIN) for tile in range(TW)]
            build_row(patch_ref, line, pieces, lane)

        def forward(row):
            pres[row % 2][...] = jnp.dot(
                w_ref[...], patch_ref[row * LINE : row * LINE + DEEP, :], preferred_element_type=F32
            )

        for line in range(1, 3):
            build(line)
        forward(0)
        if not last:
            fetch(2, part).wait()
            fetch(3, part).wait()
        for tile in range(TW):
            before_ref[tile] = cell_buf[part, tile].astype(F32).reshape(HID * ROWS, COLS)
            live = worker_ref[base + tile] >= 0
            up = grad_buf[part, tile].astype(F32).reshape(HID * ROWS, COLS)
            up_ref[tile] = jnp.where(live, up, 0.0)
        for row in range(ROWS):
            if not last and row == 1 and part == 0:
                fetch(2, 1).start()
                fetch(3, 1).start()
                fetch(0, 1).wait()
                fetch(1, 1).wait()
            if not last and row == 4 and part == 0:
                stage(1, stages[6])
                for tile in range(TW):
                    leading_1[tile] = load_rows(stages[0], tile, 0, KIN).astype(BF16)
                    ending_2[tile] = load_rows(stages[6], tile, ROWS - 1, KIN).astype(BF16)
            if not last and row == 1 and part == 1:
                for index in range(2):
                    for which in range(2):
                        fetch_ahead(which, index).start()
            if row + 1 < ROWS:
                build(row + 3)
                forward(row + 1)
            gates_of_row(pres[row % 2], before_ref, up_ref, hidden_new, cell_new, grad_ref, row)

        for tile in range(TW):
            live = worker_ref[base + tile] >= 0
            fresh = hidden_new[tile].reshape(HID, ROWS, COLS).astype(BF16)
            hidden_res[part, tile] = jnp.where(live, fresh, hidden_buf[tile])
            fresh = cell_new[tile].reshape(HID, ROWS, COLS).astype(BF16)
            cell_res[part, tile] = jnp.where(live, fresh, cell_buf[part, tile])
        flush(0, part).start()
        flush(1, part).start()
        left = jnp.concatenate([patch_ref[row * LINE : row * LINE + DEEP, :] for row in range(ROWS)], axis=1)
        product = lax.dot_general(left, grad_ref[...], (((1,), (1,)), ((), ())), preferred_element_type=F32)
        if part:
            total_ref[...] += product
        elif last:
            total_ref[...] = acc_in_ref[...] + product
        else:
            total_ref[...] = product

    run((stages[12], stages[13]), (stages[14], stages[15]))


def compute(first, step, worker, carried, hidden, last):
    resident = pl.BlockSpec(memory_space=pltpu.VMEM)
    anywhere = pl.BlockSpec(memory_space=pl.ANY)
    operands = [worker] + carried
    scalars = pl.BlockSpec(memory_space=pltpu.SMEM)
    state = jax.ShapeDtypeStruct(hidden.shape, BF16)
    small = (TW, CIN, ROWS, COLS)
    medium = (TW, HID, ROWS, COLS)
    large = (2, TW, HID, ROWS, COLS)
    out_shape = [state, state]
    aliases = {}
    scratch = []
    if last:
        in_specs = [scalars] + [resident] * 10 + [anywhere] * 2
        aliases = {11: 0, 12: 1}
        out_shape.append(jax.ShapeDtypeStruct((GATES // (2 * ROWS), ROWS, DEEP), F32))
        out_shape.append(jax.ShapeDtypeStruct((GATES // (2 * ROWS), ROWS, DEEP), BF16))
    else:
        in_specs = [scalars] + [anywhere] * 4 + [resident] * 6
        out_shape.append(jax.ShapeDtypeStruct((DEEP, GATES), F32))
        out_shape.append(jax.ShapeDtypeStruct((GATES, DEEP), BF16))
        edge = (TW, KIN, COLS)
        out_shape += [jax.ShapeDtypeStruct(shape, BF16) for shape in (edge, edge, large, large)]
        scratch = [pltpu.VMEM(shape, BF16) for shape in (small, medium, large, large)]
        scratch += [pltpu.SemaphoreType.DMA((4, 2)), pltpu.SemaphoreType.DMA((2, 2))]
    stage = pltpu.VMEM((TW, HID * ROWS, COLS), F32)
    return pl.pallas_call(
        functools.partial(compute_kernel, first, step, last),
        in_specs=in_specs,
        out_specs=[anywhere, anywhere] + [resident] * (len(out_shape) - 2),
        scratch_shapes=scratch + [
            pltpu.VMEM(large, BF16),
            pltpu.VMEM(large, BF16),
            pltpu.SemaphoreType.DMA((2, 2)),
            pltpu.VMEM((DEEP, GATES), F32),
            pltpu.VMEM((GATES, ROW), F32),
            pltpu.VMEM((GATES, ROW), F32),
            *([pltpu.VMEM((TW, KIN * ROWS, COLS), F32), stage, stage, stage, stage, pltpu.VMEM((8, 128), F32)] * 2),
            pltpu.VMEM(((ROWS + 2) * LINE, ROW), BF16), pltpu.VMEM(((ROWS + 2) * LINE, ROW), BF16), pltpu.VMEM((GATES, ROWS * ROW), BF16), pltpu.VMEM((GATES, ROWS * ROW), BF16),
        ],
        out_shape=out_shape,
        input_output_aliases=aliases,
        compiler_params=pltpu.CompilerParams(vmem_limit_bytes=40 << 20),
        cost_estimate=pl.CostEstimate(
            flops=8 * TW * ROWS * COLS * TAPS * GATES, bytes_accessed=6 << 20, transcendentals=0
        ),
        name="second" if last else "first",
    )(*operands)


def shards(forcing, hidden_prev, cell_prev, hidden_grad, w_gates, gate_bias, worker):
    size = lax.axis_size("space")
    forcing, hidden, cell, grad = [
        pltpu.with_memory_space_constraint(array[0], pltpu.HBM)
        for array in (forcing, hidden_prev, cell_prev, hidden_grad)
    ]
    near, far, ending_0, leading_3, forcing_vmem, hidden_vmem = edges(forcing, hidden)
    near_halo = lax.ppermute(near, "space", [(i, i ^ 1) for i in range(size)])
    far_pairs = [(i, i + 1) for i in range(1, size - 1, 2)]
    far_halo = lax.ppermute(far, "space", far_pairs + [(j, i) for i, j in far_pairs])
    tiles = worker[0]
    hidden_part, cell_part, total, w, leading_1, ending_2, *ahead = compute(
        1, 1, tiles,
        [forcing, hidden, cell, grad, forcing_vmem, hidden_vmem, ending_0, leading_3, w_gates.T, gate_bias[None, :]],
        hidden, False,
    )
    hidden_next, cell_next, own, other = compute(
        0, 3, tiles,
        [forcing_vmem, hidden_vmem, *ahead, near_halo, leading_1, ending_2, far_halo, w, total, hidden_part, cell_part], hidden, True,
    )
    half = own + lax.ppermute(other, "space", [(i, i ^ 1) for i in range(size)]).astype(F32)
    groups = [list(range(core, size, 2)) for core in range(2)]
    pieces = lax.all_to_all(half.astype(BF16), "space", 0, 0, tiled=True, axis_index_groups=groups)
    mine = jnp.sum(pieces.astype(F32), axis=0).astype(BF16)
    years = lax.axis_size("dp")
    total = mine.astype(F32)
    for k in range(1, years):
        other = lax.ppermute(mine, "dp", [(i, (i + k) % years) for i in range(years)])
        total = total + other.astype(F32)
    return hidden_next[None], cell_next[None], total[:, :TAPS], total[:, TAPS]


def solution(mesh):
    tiles = P("dp", "space", None, None, None)
    return jax.shard_map(
        shards,
        mesh=mesh,
        in_specs=(tiles, tiles, tiles, tiles, P(), P(), P("dp", None)),
        out_specs=(tiles, tiles, P("space", None), P("space")),
        check_vma=False,
    )
```

```python
import functools

import jax
import jax.numpy as jnp
from jax import lax
from jax.experimental import pallas as pl
from jax.experimental.pallas import tpu as pltpu
from jax.sharding import PartitionSpec as P

CIN = 16
HID = 64
KIN = CIN + HID
GATES = 4 * HID
ROWS = 8
COLS = 128
TW = 4
BAND = 4
WIDE = 3 * KIN
LINE = 256
CHUNK = 16
WHOLE = (0, ROWS)
SINGLE = tuple(range(ROWS + 1))
TAPS = 3 * WIDE
DEEP = 3 * LINE
ROW = TW * COLS

F32 = jnp.float32
BF16 = jnp.bfloat16


def load_rows(stage, tile, row, count, start=0):
    return stage[tile, pl.ds(row + start * ROWS, count, stride=ROWS), :]


def build_row(patch_ref, line, pieces, lane):
    zero = jnp.zeros((KIN, COLS), F32)
    right = [pltpu.roll(piece, 1, 1) for piece in pieces]
    left = [pltpu.roll(piece, COLS - 1, 1) for piece in pieces]
    for tile in range(TW):
        before = right[tile - 1] if tile else zero
        after = left[tile + 1] if tile < TW - 1 else zero
        shifted = (
            jnp.where(lane == 0, before, right[tile]),
            pieces[tile],
            jnp.where(lane == COLS - 1, after, left[tile]),
        )
        span = slice(tile * COLS, (tile + 1) * COLS)
        for offset, value in enumerate(shifted):
            patch_ref[line * LINE + offset * KIN : line * LINE + (offset + 1) * KIN, span] = value.astype(BF16)


def edge_kernel(forcing_hbm, hidden_hbm, near_ref, far_ref, ending_0, leading_3, forcing_buf, hidden_buf, joined_ref, sem):
    odd = lax.rem(lax.axis_index("space"), 2) == 1
    copies = []
    for slot, band_row in ((0, 0), (2, BAND - 1), (1, 1)):
        for which, (hbm, buf) in enumerate(((forcing_hbm, forcing_buf), (hidden_hbm, hidden_buf))):
            copies.append(
                pltpu.make_async_copy(hbm.at[pl.ds(band_row * TW, TW)], buf.at[slot], sem.at[which, slot])
            )
            copies[-1].start()
    for copy in copies[:4]:
        copy.wait()
    for tile in range(TW):
        for which in range(2):
            slot = which * TW + tile
            joined_ref[slot, : CIN * ROWS, :] = forcing_buf[2 * which, tile].astype(F32).reshape(CIN * ROWS, COLS)
            joined_ref[slot, CIN * ROWS :, :] = hidden_buf[2 * which, tile].astype(F32).reshape(HID * ROWS, COLS)
        first_row = load_rows(joined_ref, tile, 0, KIN)
        last_row = load_rows(joined_ref, TW + tile, ROWS - 1, KIN)
        near_ref[tile] = jnp.where(odd, first_row, last_row).astype(BF16)
        far_ref[tile] = jnp.where(odd, last_row, first_row).astype(BF16)
        ending_0[tile] = load_rows(joined_ref, tile, ROWS - 1, KIN).astype(BF16)
        leading_3[tile] = load_rows(joined_ref, TW + tile, 0, KIN).astype(BF16)
    for copy in copies[4:]:
        copy.wait()


def edges(forcing, hidden):
    shape = jax.ShapeDtypeStruct((TW, KIN, COLS), BF16)
    return pl.pallas_call(
        edge_kernel,
        in_specs=[pl.BlockSpec(memory_space=pl.ANY)] * 2,
        out_specs=[pl.BlockSpec(memory_space=pltpu.VMEM)] * 6,
        out_shape=[shape] * 4 + [jax.ShapeDtypeStruct((3, TW, n, ROWS, COLS), BF16) for n in (CIN, HID)],
        scratch_shapes=[pltpu.VMEM((2 * TW, KIN * ROWS, COLS), F32), pltpu.SemaphoreType.DMA((2, 3))],
        compiler_params=pltpu.CompilerParams(vmem_limit_bytes=24 << 20),
        cost_estimate=pl.CostEstimate(flops=0, bytes_accessed=3 << 20, transcendentals=0),
        name="edges",
    )(forcing, hidden)


def prepare(weight_ref, bias_ref, w_ref, wide_ref):
    wide_ref[...] = jnp.zeros((DEEP, GATES), F32)
    for tap in range(3):
        wide_ref[tap * LINE : tap * LINE + WIDE, :] = weight_ref[tap * WIDE : (tap + 1) * WIDE, :].astype(F32)
    rest = bias_ref[...]
    for piece in range(3):
        value = rest.astype(BF16).astype(F32)
        wide_ref[WIDE + piece : WIDE + piece + 1, :] = value
        rest = rest - value
    gate = lax.broadcasted_iota(jnp.int32, (GATES, 1), 0)
    w_ref[...] = (wide_ref[...].T * jnp.where(gate < 3 * HID, 0.5, 1.0)).astype(BF16)


def fill_ones(patch_ref):
    index = lax.broadcasted_iota(jnp.int32, (LINE - WIDE, ROW), 0)
    ones = jnp.where(index < 3, 1.0, 0.0).astype(BF16)
    for line in range(ROWS + 2):
        patch_ref[line * LINE + WIDE : (line + 1) * LINE, :] = ones


def gates_of_row(pre_ref, before_ref, up_ref, hidden_new, cell_new, grad_ref, row):
    for tile in range(TW):
        span = slice(tile * COLS, (tile + 1) * COLS)
        out_span = slice(row * ROW + tile * COLS, row * ROW + (tile + 1) * COLS)
        for start in range(0, HID, CHUNK):
            in_half, forget_half, out_half, candidate = [
                jnp.tanh(pre_ref[k * HID + start : k * HID + start + CHUNK, span]) for k in range(4)
            ]
            in_gate, forget_gate, out_gate = [0.5 * half + 0.5 for half in (in_half, forget_half, out_half)]
            cell_before = load_rows(before_ref, tile, row, CHUNK, start)
            upstream = load_rows(up_ref, tile, row, CHUNK, start)
            kept = forget_gate * cell_before
            cell_full = kept + in_gate * candidate
            squashed = jnp.tanh(cell_full)
            place = pl.ds(row + start * ROWS, CHUNK, stride=ROWS)
            hidden_new[tile, place, :] = out_gate * squashed
            cell_new[tile, place, :] = cell_full
            raised = upstream * out_gate
            d_cell = raised * (1.0 - squashed * squashed)
            d_in = d_cell * in_gate
            parts = [
                d_in * candidate * (1.0 - in_gate),
                d_cell * kept * (1.0 - forget_gate),
                raised * squashed * (1.0 - out_gate),
                d_in * (1.0 - candidate * candidate),
            ]
            for k, part in enumerate(parts):
                grad_ref[k * HID + start : k * HID + start + CHUNK, out_span] = part.astype(BF16)


def compute_kernel(
    first, step, last,
    worker_ref,
    *rest,
):
    if last:
        (forcing_in, hidden_in, cell_buf, grad_buf, near_halo, leading_1, ending_2, far_halo,
         w_ref, acc_in_ref, _, _, hidden_hbm_out, cell_hbm_out, own_out, other_out) = rest[:16]
        scratch = rest[16:]
        state_of = [(forcing_in.at[2 * part], hidden_in.at[2 * part]) for part in range(2)]
    else:
        sources = rest[:4]
        (forcing_in, hidden_in, ending_0, leading_3, weight_ref, bias_ref,
         hidden_hbm_out, cell_hbm_out, sum_out, w_ref, leading_1, ending_2) = rest[4:16]
        ahead = rest[16:18]
        (forcing_own, hidden_own, cell_buf, grad_buf, in_sem, ahead_sem) = rest[18:24]
        scratch = rest[24:]
        state_of = [(forcing_in.at[1], hidden_in.at[1]), (forcing_own, hidden_own)]
    hidden_res, cell_res, out_sem, total_ref, pre_a, pre_b = scratch[:6]
    stages = scratch[6:]
    home = lax.axis_index("space")
    odd = lax.rem(home, 2) == 1
    pres = (pre_a, pre_b)

    def fetch(which, index):
        buffer = (forcing_own, hidden_own, cell_buf.at[index], grad_buf.at[index])[which]
        return pltpu.make_async_copy(
            sources[which].at[pl.ds((first + index * step) * TW, TW)], buffer, in_sem.at[which, index]
        )

    def fetch_ahead(which, index):
        return pltpu.make_async_copy(
            sources[which + 2].at[pl.ds(index * (BAND - 1) * TW, TW)], ahead[which].at[index], ahead_sem.at[which, index]
        )

    def flush(which, index):
        hbm, buf = ((hidden_hbm_out, hidden_res), (cell_hbm_out, cell_res))[which]
        return pltpu.make_async_copy(
            buf.at[index], hbm.at[pl.ds((first + index * step) * TW, TW)], out_sem.at[which, index]
        )

    def run(patches, grads):
        if not last:
            for which, index in ((2, 0), (3, 0), (0, 1), (1, 1)):
                fetch(which, index).start()
        for patch_ref in patches:
            fill_ones(patch_ref)
        if not last:
            prepare(weight_ref, bias_ref, w_ref, total_ref)
        waiting = []
        for part in range(2):
            one_part(part, patches, grads, waiting, stages[0], *stages[6 * part : 6 * part + 6])
        backward(waiting, patches, grads)
        if last:
            packed = jnp.concatenate(
                [total_ref[tap * LINE : tap * LINE + WIDE, :] for tap in range(3)]
                + [total_ref[WIDE:LINE, :], jnp.zeros((DEEP - TAPS - LINE + WIDE, GATES), F32)],
                axis=0,
            )
            turned = packed.T
            for pair in range(GATES // (2 * ROWS)):
                even_half = turned[2 * pair * ROWS : (2 * pair + 1) * ROWS]
                odd_half = turned[(2 * pair + 1) * ROWS : (2 * pair + 2) * ROWS]
                own_out[pair] = jnp.where(odd, odd_half, even_half)
                other_out[pair] = jnp.where(odd, even_half, odd_half).astype(BF16)
        else:
            sum_out[...] = total_ref[...]
            for index in range(2):
                for which in range(2):
                    fetch_ahead(which, index).wait()
        for index in range(2):
            for which in range(2):
                flush(which, index).wait()

    def backward(waiting, patches, grads):
        if not waiting:
            return
        part, start, stop = waiting.pop()
        rows = range(start, stop)
        left = jnp.concatenate([patches[part][row * LINE : row * LINE + DEEP, :] for row in rows], axis=1)
        right = grads[part][:, start * ROW : stop * ROW]
        product = lax.dot_general(left, right, (((1,), (1,)), ((), ())), preferred_element_type=F32)
        if part or start:
            total_ref[...] += product
        elif last:
            total_ref[...] = acc_in_ref[...] + product
        else:
            total_ref[...] = product

    def one_part(part, patches, grads, waiting, joined_0, joined_ref, before_ref, up_ref, hidden_new, cell_new, _):
        patch_ref, grad_ref = patches[part], grads[part]
        cuts = SINGLE if last else WHOLE
        base = home * (BAND * TW) + (first + part * step) * TW
        forcing_buf, hidden_buf = state_of[part]
        lane = lax.broadcasted_iota(jnp.int32, (KIN, COLS), 1)

        def stage(which, into):
            forcing_ref, hidden_ref = state_of[which]
            for tile in range(TW):
                into[tile, : CIN * ROWS, :] = forcing_ref[tile].astype(F32).reshape(CIN * ROWS, COLS)
                into[tile, CIN * ROWS :, :] = hidden_ref[tile].astype(F32).reshape(HID * ROWS, COLS)

        if last or part == 0:
            stage(part, joined_ref)

        def halo(even_ref, odd_ref):
            return [jnp.where(odd, odd_ref[t].astype(F32), even_ref[t].astype(F32)) for t in range(TW)]

        def plain(ref):
            return [ref[t].astype(F32) for t in range(TW)]

        if last:
            above = plain(ending_2) if part else halo(far_halo, near_halo)
            below = halo(near_halo, far_halo) if part else plain(leading_1)
        else:
            above = None if part else plain(ending_0)
            below = plain(leading_3) if part else None
        if above is None:
            patch_ref[:WIDE, :] = patches[0][ROWS * LINE : ROWS * LINE + WIDE, :]
        else:
            build_row(patch_ref, 0, above, lane)

        def build(line):
            if line == ROWS + 1 and below is None:
                pieces = [load_rows(stages[6], tile, 0, KIN) for tile in range(TW)]
            elif line == ROWS + 1:
                pieces = below
            else:
                pieces = [load_rows(joined_ref, tile, line - 1, KIN) for tile in range(TW)]
            build_row(patch_ref, line, pieces, lane)

        def forward(row):
            pres[row % 2][...] = jnp.dot(
                w_ref[...], patch_ref[row * LINE : row * LINE + DEEP, :], preferred_element_type=F32
            )

        for line in range(1, 3):
            build(line)
        forward(0)
        def state_rows():
            if not last:
                fetch(2, part).wait()
                fetch(3, part).wait()
            for tile in range(TW):
                before_ref[tile] = cell_buf[part, tile].astype(F32).reshape(HID * ROWS, COLS)
                live = worker_ref[base + tile] >= 0
                up = grad_buf[part, tile].astype(F32).reshape(HID * ROWS, COLS)
                up_ref[tile] = jnp.where(live, up, 0.0)

        for row in range(ROWS):
            if not last and row == 1 and part == 0:
                fetch(2, 1).start()
                fetch(3, 1).start()
                fetch(0, 1).wait()
                fetch(1, 1).wait()
            if not last and row == 4 and part == 0:
                stage(1, stages[6])
                for tile in range(TW):
                    leading_1[tile] = load_rows(stages[0], tile, 0, KIN).astype(BF16)
                    ending_2[tile] = load_rows(stages[6], tile, ROWS - 1, KIN).astype(BF16)
            if not last and row == 1 and part == 1:
                for index in range(2):
                    for which in range(2):
                        fetch_ahead(which, index).start()
            if row + 1 < ROWS:
                build(row + 3)
                forward(row + 1)
            if row == 0:
                state_rows()
            backward(waiting, patches, grads)
            gates_of_row(pres[row % 2], before_ref, up_ref, hidden_new, cell_new, grad_ref, row)
            for start, stop in zip(cuts, cuts[1:]):
                if row + 1 == stop:
                    waiting.append((part, start, stop))

        for tile in range(TW):
            live = worker_ref[base + tile] >= 0
            fresh = hidden_new[tile].reshape(HID, ROWS, COLS).astype(BF16)
            hidden_res[part, tile] = jnp.where(live, fresh, hidden_buf[tile])
            fresh = cell_new[tile].reshape(HID, ROWS, COLS).astype(BF16)
            cell_res[part, tile] = jnp.where(live, fresh, cell_buf[part, tile])
        flush(0, part).start()
        flush(1, part).start()
        if not last:
            backward(waiting, patches, grads)

    run((stages[12], stages[13]), (stages[14], stages[15]))


def compute(first, step, worker, carried, hidden, last):
    resident = pl.BlockSpec(memory_space=pltpu.VMEM)
    anywhere = pl.BlockSpec(memory_space=pl.ANY)
    operands = [worker] + carried
    scalars = pl.BlockSpec(memory_space=pltpu.SMEM)
    state = jax.ShapeDtypeStruct(hidden.shape, BF16)
    small = (TW, CIN, ROWS, COLS)
    medium = (TW, HID, ROWS, COLS)
    large = (2, TW, HID, ROWS, COLS)
    out_shape = [state, state]
    aliases = {}
    scratch = []
    if last:
        in_specs = [scalars] + [resident] * 10 + [anywhere] * 2
        aliases = {11: 0, 12: 1}
        out_shape.append(jax.ShapeDtypeStruct((GATES // (2 * ROWS), ROWS, DEEP), F32))
        out_shape.append(jax.ShapeDtypeStruct((GATES // (2 * ROWS), ROWS, DEEP), BF16))
    else:
        in_specs = [scalars] + [anywhere] * 4 + [resident] * 6
        out_shape.append(jax.ShapeDtypeStruct((DEEP, GATES), F32))
        out_shape.append(jax.ShapeDtypeStruct((GATES, DEEP), BF16))
        edge = (TW, KIN, COLS)
        out_shape += [jax.ShapeDtypeStruct(shape, BF16) for shape in (edge, edge, large, large)]
        scratch = [pltpu.VMEM(shape, BF16) for shape in (small, medium, large, large)]
        scratch += [pltpu.SemaphoreType.DMA((4, 2)), pltpu.SemaphoreType.DMA((2, 2))]
    stage = pltpu.VMEM((TW, HID * ROWS, COLS), F32)
    return pl.pallas_call(
        functools.partial(compute_kernel, first, step, last),
        in_specs=in_specs,
        out_specs=[anywhere, anywhere] + [resident] * (len(out_shape) - 2),
        scratch_shapes=scratch + [
            pltpu.VMEM(large, BF16),
            pltpu.VMEM(large, BF16),
            pltpu.SemaphoreType.DMA((2, 2)),
            pltpu.VMEM((DEEP, GATES), F32),
            pltpu.VMEM((GATES, ROW), F32),
            pltpu.VMEM((GATES, ROW), F32),
            *([pltpu.VMEM((TW, KIN * ROWS, COLS), F32), stage, stage, stage, stage, pltpu.VMEM((8, 128), F32)] * 2),
            pltpu.VMEM(((ROWS + 2) * LINE, ROW), BF16), pltpu.VMEM(((ROWS + 2) * LINE, ROW), BF16), pltpu.VMEM((GATES, ROWS * ROW), BF16), pltpu.VMEM((GATES, ROWS * ROW), BF16),
        ],
        out_shape=out_shape,
        input_output_aliases=aliases,
        compiler_params=pltpu.CompilerParams(vmem_limit_bytes=40 << 20),
        cost_estimate=pl.CostEstimate(
            flops=8 * TW * ROWS * COLS * TAPS * GATES, bytes_accessed=6 << 20, transcendentals=0
        ),
        name="second" if last else "first",
    )(*operands)


def shards(forcing, hidden_prev, cell_prev, hidden_grad, w_gates, gate_bias, worker):
    size = lax.axis_size("space")
    forcing, hidden, cell, grad = [
        pltpu.with_memory_space_constraint(array[0], pltpu.HBM)
        for array in (forcing, hidden_prev, cell_prev, hidden_grad)
    ]
    near, far, ending_0, leading_3, forcing_vmem, hidden_vmem = edges(forcing, hidden)
    near_halo = lax.ppermute(near, "space", [(i, i ^ 1) for i in range(size)])
    far_pairs = [(i, i + 1) for i in range(1, size - 1, 2)]
    far_halo = lax.ppermute(far, "space", far_pairs + [(j, i) for i, j in far_pairs])
    tiles = worker[0]
    hidden_part, cell_part, total, w, leading_1, ending_2, *ahead = compute(
        1, 1, tiles,
        [forcing, hidden, cell, grad, forcing_vmem, hidden_vmem, ending_0, leading_3, w_gates.T, gate_bias[None, :]],
        hidden, False,
    )
    hidden_next, cell_next, own, other = compute(
        0, 3, tiles,
        [forcing_vmem, hidden_vmem, *ahead, near_halo, leading_1, ending_2, far_halo, w, total, hidden_part, cell_part], hidden, True,
    )
    half = own + lax.ppermute(other, "space", [(i, i ^ 1) for i in range(size)]).astype(F32)
    groups = [list(range(core, size, 2)) for core in range(2)]
    pieces = lax.all_to_all(half.astype(BF16), "space", 0, 0, tiled=True, axis_index_groups=groups)
    mine = jnp.sum(pieces.astype(F32), axis=0).astype(BF16)
    years = lax.axis_size("dp")
    total = mine.astype(F32)
    for k in [years // 2] + [k for k in range(1, years) if k != years // 2]:
        other = lax.ppermute(mine, "dp", [(i, (i + k) % years) for i in range(years)])
        total = total + other.astype(F32)
    return hidden_next[None], cell_next[None], total[:, :TAPS], total[:, TAPS]


def solution(mesh):
    tiles = P("dp", "space", None, None, None)
    return jax.shard_map(
        shards,
        mesh=mesh,
        in_specs=(tiles, tiles, tiles, tiles, P(), P(), P("dp", None)),
        out_specs=(tiles, tiles, P("space", None), P("space")),
        check_vma=False,
    )
```
